32 devices in a mesh: seq: 8 (over z, y), chan: 4 (over x, core).
Axes of the slice: x: 2, y: 2, z: 4, core: 2. Of those that a mesh axis runs over, the one named last changes fastest.
Arguments:
- gate_query: bfloat16 [4096, 4096], P('seq', 'chan'), may hold values from -6 to 6
- key_input: bfloat16 [4096, 4096], P('seq', 'chan'), may hold values from -6 to 6
- value_input: bfloat16 [4096, 4096], P('seq', 'chan'), may hold values from -6 to 6
- long_filter: bfloat16 [4096, 4096], P('seq', 'chan'), may hold values from -0.09375 to 0.09375
- skip_gain: float32 [4096], P('chan'), may hold values from -4 to 4
- out_weight: bfloat16 [4096, 4096], P('chan'), may hold values from -0.09375 to 0.09375
Outputs:
- layer_out: bfloat16 [4096, 4096], P('seq', 'chan')
The draws below stay inside these ranges and needn't reach their ends.
All inputs are finite; a program needn't handle non-finite values.
Results may differ from the reference program's by a relative error of at most 0.02.
Values may be sent and summed in bfloat16 or wider, within the bound.
A program may use at most 128 MiB of HBM per device.

```python
import jax
import jax.numpy as jnp
from jax import lax

D = 4096
SEQ = 4096


def level_of(stream_key, extent, pieces, low, largest):
    factor_of, own = 1.0, jax.random.fold_in(stream_key, 6)
    for axis_at, shards_of in pieces:
        draws = jnp.exp(jax.random.uniform(jax.random.fold_in(own, axis_at), (shards_of,), jnp.float32, low / len(pieces), largest / len(pieces)))
        factor_of = factor_of * jnp.repeat(draws, extent[axis_at] // shards_of).reshape([-1 if axis == axis_at else 1 for axis in range(len(extent))])
    return factor_of


def scatter_about(key, dims, spread, most, pieces=(), dtype=jnp.bfloat16):
    level = level_of(key, dims, pieces, -0.22, 0.18) if pieces else 1.0
    array = jax.random.normal(key, dims, jnp.float32) * spread * level
    return jnp.minimum(jnp.maximum(array, -most), most).astype(dtype)


def setup_inputs(seed: int = 0) -> dict:
    arg_keys = jax.random.split(jax.random.key(seed), 7)
    return {
        "gate_query": scatter_about(arg_keys[0], (SEQ, D), 1.0, 6.0, ((0, 8), (1, 4))),
        "key_input": scatter_about(arg_keys[1], (SEQ, D), 1.0, 6.0, ((0, 8), (1, 4))),
        "value_input": scatter_about(arg_keys[2], (SEQ, D), 1.0, 6.0, ((0, 8), (1, 4))),
        "long_filter": scatter_about(arg_keys[3], (SEQ, D), SEQ ** -0.5, 0.09375, ((0, 8), (1, 4))),
        "skip_gain": scatter_about(arg_keys[4], (D,), 1.0, 4.0, ((0, 4),), jnp.float32),
        "out_weight": scatter_about(arg_keys[5], (D, D), D ** -0.5, 0.09375, ((0, 4),)),
    }


def reference(gate_query, key_input, value_input, long_filter, skip_gain, out_weight):
    signal = (key_input.astype(jnp.float32) * value_input.astype(jnp.float32)).astype(jnp.bfloat16)
    block_width = 128 if D % 128 == 0 else D
    block_count = D // block_width
    signal_blocks = signal.astype(jnp.float32).reshape(SEQ, block_count, block_width).transpose(1, 0, 2)
    filter_blocks = long_filter.astype(jnp.float32).reshape(SEQ, block_count, block_width).transpose(1, 0, 2)

    def convolve(inputs):
        signal_part, filter_part = inputs
        spectrum = jnp.fft.rfft(signal_part, n=2 * SEQ, axis=0) * jnp.fft.rfft(filter_part, n=2 * SEQ, axis=0)
        return jnp.fft.irfft(spectrum, n=2 * SEQ, axis=0)[:SEQ]

    conv = lax.map(convolve, (signal_blocks, filter_blocks)).transpose(1, 0, 2).reshape(SEQ, D)
    gated = (gate_query.astype(jnp.float32) * (conv + skip_gain[None, :] * signal.astype(jnp.float32))).astype(jnp.bfloat16)
    output = jnp.dot(gated.astype(jnp.float32), out_weight.astype(jnp.float32), preferred_element_type=jnp.float32)
    return output.astype(jnp.bfloat16)
```

```python
import functools
import math

import jax
import jax.numpy as jnp
import numpy as np
from jax import lax
from jax.experimental import pallas as pl
from jax.experimental.pallas import tpu as pltpu
from jax.sharding import PartitionSpec as P

f32 = jnp.float32
bf16 = jnp.bfloat16


def twiddles(numerator, modulus):
    angles = 2.0 * math.pi / modulus * (numerator % modulus).astype(f32)
    return jnp.cos(angles), jnp.sin(angles)


def convolve(signal, long_filter):
    groups = lax.axis_size("seq")
    seq_len, channels = signal.shape
    padded = 2 * groups * seq_len
    own = channels // groups
    stacked = jnp.stack([long_filter, signal])
    got = lax.all_to_all(stacked, "seq", split_axis=2, concat_axis=1, tiled=True)
    blocks = got.reshape(2, groups, seq_len, own)
    classes = jnp.arange(groups + 1, dtype=jnp.int32)
    devs = jnp.arange(groups, dtype=jnp.int32)
    offsets = jnp.arange(seq_len, dtype=jnp.int32)
    cos_dev, sin_dev = twiddles(classes[:, None] * devs[None, :], 2 * groups)
    cos_tw, sin_tw = twiddles(classes[:, None] * offsets[None, :], padded)
    cos_tw, sin_tw = cos_tw[:, :, None], sin_tw[:, :, None]
    cos_seq, sin_seq = twiddles(offsets[:, None] * offsets[None, :], seq_len)
    fourier = jnp.concatenate(
        [
            jnp.concatenate([cos_seq, sin_seq], axis=1),
            jnp.concatenate([-sin_seq, cos_seq], axis=1),
        ],
        axis=0,
    ).astype(bf16)
    real = jnp.einsum("kd,sdmc->skmc", cos_dev.astype(bf16), blocks, preferred_element_type=f32)
    imag = -jnp.einsum("kd,sdmc->skmc", sin_dev.astype(bf16), blocks, preferred_element_type=f32)
    turned = jnp.concatenate(
        [real * cos_tw + imag * sin_tw, imag * cos_tw - real * sin_tw], axis=2
    ).astype(bf16)
    spectra = jnp.einsum("ab,skbc->skac", fourier, turned, preferred_element_type=f32)
    f_re, f_im = spectra[0, :, :seq_len], spectra[0, :, seq_len:]
    s_re, s_im = spectra[1, :, :seq_len], spectra[1, :, seq_len:]
    prod = jnp.concatenate(
        [f_re * s_re - f_im * s_im, -(f_re * s_im + f_im * s_re)], axis=1
    ).astype(bf16)
    back = jnp.einsum("ab,kbc->kac", fourier, prod, preferred_element_type=f32)
    b_re, b_im = back[:, :seq_len], -back[:, seq_len:]
    r_re = (b_re * cos_tw - b_im * sin_tw).astype(bf16)
    r_im = (b_re * sin_tw + b_im * cos_tw).astype(bf16)
    weight = jnp.where((classes == 0) | (classes == groups), 1.0, 2.0)[:, None]
    conv = jnp.einsum(
        "kd,kmc->dmc", (cos_dev * weight).astype(bf16), r_re, preferred_element_type=f32
    ) - jnp.einsum(
        "kd,kmc->dmc", (sin_dev * weight).astype(bf16), r_im, preferred_element_type=f32
    )
    conv = (conv * (1.0 / padded)).astype(bf16).reshape(groups * seq_len, own)
    return lax.all_to_all(conv, "seq", split_axis=0, concat_axis=1, tiled=True).astype(f32)


LANES = 128
AHEAD = 3
PARTS = (4, 4, 4, 4, 4, 4, 4, 4)


def layer_kernel(
    sizes,
    gate_hbm, key_hbm, value_hbm, filt_hbm, skip_ref, weight_hbm, forward_hbm, inverse_hbm,
    out_hbm,
    gate, key, value, weight, forward, inverse,
    filt_in, sig_in, sig, filt_spec, sig_spec, prod, conv_out, conv_in, gated,
    own, pair_out, pair_in, cross_out, cross_in, result,
    load_sem, fsend, frecv, ssend, srecv, csend, crecv, psend, precv, xsend, xrecv, store_sem,
):
    groups, rows = filt_in.shape[0], filt_in.shape[1]
    me = lax.axis_index("seq")
    chan = lax.axis_index("chan")
    core = lax.rem(chan, 2)
    side = chan // 2
    pair = chan + 1 - 2 * core
    cross = lax.rem(chan + 2, 4)
    columns = weight.shape[2]
    chunks = len(sizes)
    starts = [sum(sizes[:q]) for q in range(chunks)]
    peers = [lax.rem(me + j, groups) for j in range(groups)]
    origins = [lax.rem(me + groups - j, groups) for j in range(groups)]

    def load(src, dst, at):
        copy = pltpu.make_async_copy(src, dst, load_sem.at[at])
        copy.start()
        return copy

    def lanes_of(p):
        return pl.ds(pl.multiple_of(p * LANES, LANES), LANES)

    key_load = load(key_hbm, key, 0)
    value_load = load(value_hbm, value, 1)

    barrier = pltpu.get_barrier_semaphore()
    for j in range(1, groups):
        pl.semaphore_signal(barrier, inc=1, device_id={"seq": peers[j]}, device_id_type=pl.DeviceIdType.MESH)
    for other in (pair, cross):
        pl.semaphore_signal(barrier, inc=1, device_id={"chan": other}, device_id_type=pl.DeviceIdType.MESH)
    pl.semaphore_wait(barrier, groups + 1)

    def remote(src, dst, send, recv, where):
        copy = pltpu.make_async_remote_copy(
            src_ref=src, dst_ref=dst, send_sem=send, recv_sem=recv,
            device_id=where, device_id_type=pl.DeviceIdType.MESH,
        )
        copy.start()
        return copy

    filt_copies = [
        remote(filt_hbm.at[:, lanes_of(peers[j])], filt_in.at[me], fsend.at[j], frecv.at[j], {"seq": peers[j]})
        for j in range(1, groups)
    ]
    key_load.wait()
    value_load.wait()

    def multiply(i, _):
        at = pl.ds(i * 32, 32)
        for p in range(groups):
            cols = slice(p * LANES, (p + 1) * LANES)
            sig[p, at, :] = (key[at, cols].astype(f32) * value[at, cols].astype(f32)).astype(bf16)
        return 0

    lax.fori_loop(0, rows // 32, multiply, 0)
    sig_copies = [
        remote(sig.at[peers[j]], sig_in.at[me], ssend.at[j], srecv.at[j], {"seq": peers[j]})
        for j in range(1, groups)
    ]
    filt_own = load(filt_hbm.at[:, lanes_of(me)], filt_in.at[me], 2)
    forward_load = load(forward_hbm, forward, 3)
    late = [load(inverse_hbm, inverse, 4), load(gate_hbm, gate, 5)] + [
        load(weight_hbm.at[:, pl.ds(b * columns, columns)], weight.at[b], 6 + b) for b in range(4)
    ]
    sig_in[me] = sig[me]

    def transform(src, spec, first, second):
        def body(i, _):
            at = pl.ds(i * 256, 256)
            both = jnp.concatenate([src[first], src[second]], axis=1)
            acc = jnp.dot(forward[at, :], both, preferred_element_type=f32)
            spec[first, at, :] = acc[:, :LANES]
            spec[second, at, :] = acc[:, LANES:]
            return 0

        lax.fori_loop(0, 2 * rows // 256, body, 0)

    def transform_all(src, spec, copies):
        for j in range(0, groups, 2):
            for copy in copies[max(j - 1, 0) : j + 1]:
                copy.wait_recv()
            transform(src, spec, origins[j], origins[j + 1])

    forward_load.wait()
    filt_own.wait()
    transform_all(filt_in, filt_spec, filt_copies)
    scale = 1.0 / rows

    def overlap(i, _):
        for first, sign in ((0, 1.0), (rows // 2, -1.0)):
            at = pl.ds(first + i * 8, 8)
            low = pl.ds(rows + first + i * 8, 8)
            last_re, last_im = None, None
            for j in range(groups):
                re, im = filt_spec[j, at, :] * scale, filt_spec[j, low, :] * scale
                if j == 0:
                    filt_spec[j, at, :], filt_spec[j, low, :] = re, im
                else:
                    filt_spec[j, at, :] = re - sign * last_im
                    filt_spec[j, low, :] = im + sign * last_re
                last_re, last_im = re, im
        return 0

    lax.fori_loop(0, rows // 16, overlap, 0)
    transform_all(sig_in, sig_spec, sig_copies)

    def multiply_spectra(i, _):
        at = pl.ds(i * 16, 16)
        low = pl.ds(rows + i * 16, 16)
        for n in range(groups):
            re, im = None, None
            for j in range(n + 1):
                f_re, f_im = filt_spec[j, at, :], filt_spec[j, low, :]
                s_re, s_im = sig_spec[n - j, at, :], sig_spec[n - j, low, :]
                t_re, t_im = f_re * s_re - f_im * s_im, f_re * s_im + f_im * s_re
                re, im = (t_re, t_im) if j == 0 else (re + t_re, im + t_im)
            cols = slice(n * LANES, (n + 1) * LANES)
            prod[at, cols] = re.astype(bf16)
            prod[low, cols] = im.astype(bf16)
        return 0

    lax.fori_loop(0, rows // 16, multiply_spectra, 0)
    for copy in late:
        copy.wait()

    conv_copies = []

    def send_conv(q):
        span = pl.ds(starts[q], sizes[q])
        back = jnp.dot(inverse[span, :], prod[...], preferred_element_type=f32)
        for d in range(groups):
            conv_out[d, span, :] = back[:, d * LANES : (d + 1) * LANES].astype(bf16)
        conv_copies.append(
            [
                remote(
                    conv_out.at[peers[j], span], conv_in.at[me, span],
                    csend.at[q, j], crecv.at[q, j], {"seq": peers[j]},
                )
                for j in range(1, groups)
            ]
        )
        conv_in[me, span, :] = conv_out[me, span, :]

    for q in range(min(AHEAD, chunks)):
        send_conv(q)

    pair_copies, cross_copies, stores = [], [], []
    there, here = 1 - side, side

    def project(q, x, is_pair):
        chunk, span = sizes[q], pl.ds(starts[q], sizes[q])
        part = jnp.dot(
            gated[:chunk, :],
            weight[2 * x + (1 - core if is_pair else core)],
            preferred_element_type=f32,
        )
        if not is_pair:
            own[x, span, :] = part
            return
        pair_out[x, span, :] = part.astype(bf16)
        at = 2 * q + (0 if x is there else 1)
        pair_copies.append(
            remote(
                pair_out.at[x, span], pair_in.at[x, span],
                psend.at[at], precv.at[at], {"chan": pair},
            )
        )

    def finish(q):
        span = pl.ds(starts[q], sizes[q])
        cross_copies[q].wait_recv()
        result[span, :] = (own[here, span, :] + cross_in[span, :].astype(f32)).astype(bf16)
        copy = pltpu.make_async_copy(result.at[span], out_hbm.at[span], store_sem.at[q])
        copy.start()
        stores.append(copy)

    for q in range(chunks):
        for copy in conv_copies[q]:
            copy.wait_recv()
        chunk = sizes[q]
        rows_q = slice(starts[q], starts[q] + chunk)
        span = pl.ds(starts[q], chunk)
        for s in range(groups):
            cols = slice(s * LANES, (s + 1) * LANES)
            mixed = conv_in[s, rows_q, :].astype(f32) + skip_ref[:, cols] * sig[s, rows_q, :].astype(f32)
            gated[:chunk, cols] = (gate[rows_q, cols].astype(f32) * mixed).astype(bf16)
        project(q, there, True)
        project(q, there, False)
        project(q, here, True)
        pair_copies[2 * q].wait_recv()
        cross_out[span, :] = (own[there, span, :] + pair_in[there, span, :].astype(f32)).astype(bf16)
        cross_copies.append(
            remote(cross_out.at[span], cross_in.at[span], xsend.at[q], xrecv.at[q], {"chan": cross})
        )
        project(q, here, False)
        if q + AHEAD < chunks:
            send_conv(q + AHEAD)
        pair_copies[2 * q + 1].wait_recv()
        own[here, span, :] = own[here, span, :] + pair_in[here, span, :].astype(f32)
        if q >= 2:
            finish(q - 2)
    for q in range(max(chunks - 2, 0), chunks):
        finish(q)

    for copy in filt_copies + sig_copies + pair_copies + cross_copies:
        copy.wait_send()
    for copies in conv_copies:
        for copy in copies:
            copy.wait_send()
    for copy in stores:
        copy.wait()


def transform_matrices(rows):
    freq = np.concatenate([np.arange(0, rows, 2), np.arange(1, rows, 2)])
    numerator = ((2 * freq[:, None] + 1) * np.arange(rows)[None, :]) % (4 * rows)
    angle = np.pi / (2 * rows) * numerator
    forward = np.concatenate([np.cos(angle), -np.sin(angle)], axis=0)
    return forward.astype(jnp.bfloat16), np.ascontiguousarray(forward.T).astype(jnp.bfloat16)


def fused(gate_query, key_input, value_input, long_filter, skip_gain, out_weight, sizes):
    groups = lax.axis_size("seq")
    rows, channels = gate_query.shape
    columns = out_weight.shape[1] // 4
    chunks, chunk = len(sizes), max(sizes)
    forward, inverse = transform_matrices(rows)
    blocks = (groups, rows, LANES)
    spectra = (groups, 2 * rows, LANES)
    dma = pltpu.SemaphoreType.DMA
    anywhere = pl.BlockSpec(memory_space=pl.ANY)
    in_vmem = pl.BlockSpec(memory_space=pltpu.VMEM)
    return pl.pallas_call(
        functools.partial(layer_kernel, sizes),
        out_shape=jax.ShapeDtypeStruct((rows, columns), bf16),
        in_specs=[anywhere] * 4 + [in_vmem] + [anywhere] * 3,
        out_specs=anywhere,
        scratch_shapes=[
            pltpu.VMEM((rows, channels), bf16),
            pltpu.VMEM((rows, channels), bf16),
            pltpu.VMEM((rows, channels), bf16),
            pltpu.VMEM((4, channels, columns), bf16),
            pltpu.VMEM((2 * rows, rows), bf16),
            pltpu.VMEM((rows, 2 * rows), bf16),
            pltpu.VMEM(blocks, bf16),
            pltpu.VMEM(blocks, bf16),
            pltpu.VMEM(blocks, bf16),
            pltpu.VMEM(spectra, f32),
            pltpu.VMEM(spectra, f32),
            pltpu.VMEM((2 * rows, groups * LANES), bf16),
            pltpu.VMEM(blocks, bf16),
            pltpu.VMEM(blocks, bf16),
            pltpu.VMEM((chunk, channels), bf16),
            pltpu.VMEM((2, rows, columns), f32),
            pltpu.VMEM((2, rows, columns), bf16),
            pltpu.VMEM((2, rows, columns), bf16),
            pltpu.VMEM((rows, columns), bf16),
            pltpu.VMEM((rows, columns), bf16),
            pltpu.VMEM((rows, columns), bf16),
            dma((10,)),
            dma((groups,)),
            dma((groups,)),
            dma((groups,)),
            dma((groups,)),
            dma((chunks, groups)),
            dma((chunks, groups)),
            dma((2 * chunks,)),
            dma((2 * chunks,)),
            dma((chunks,)),
            dma((chunks,)),
            dma((chunks,)),
        ],
        compiler_params=pltpu.CompilerParams(
            collective_id=0, has_side_effects=True, vmem_limit_bytes=60 * 1024 * 1024
        ),
        name="layer",
    )(
        gate_query, key_input, value_input, long_filter, skip_gain[None, :], out_weight,
        jnp.asarray(forward), jnp.asarray(inverse),
    )


def chunk_sizes(rows):
    return tuple(rows * part // sum(PARTS) for part in PARTS)


def groups_fit(block, weight, chans):
    rows, channels = block
    return (
        lax.axis_size("seq") == 8
        and chans == 4
        and channels == 8 * LANES
        and rows % 256 == 0
        and rows <= 512
        and weight[1] % (4 * LANES) == 0
        and weight[1] <= 4096
    )


def shards(gate_query, key_input, value_input, long_filter, skip_gain, out_weight):
    chans = lax.axis_size("chan")
    if groups_fit(gate_query.shape, out_weight.shape, chans):
        return fused(
            gate_query, key_input, value_input, long_filter, skip_gain, out_weight, chunk_sizes(gate_query.shape[0])
        )
    signal = (key_input.astype(f32) * value_input.astype(f32)).astype(bf16)
    conv = convolve(signal, long_filter)
    gated = (
        gate_query.astype(f32) * (conv + skip_gain[None, :] * signal.astype(f32))
    ).astype(bf16)
    summed = lax.psum_scatter(
        lax.dot_general(
            out_weight, gated, (((0,), (1,)), ((), ())), preferred_element_type=f32
        ).astype(bf16),
        "chan",
        scatter_dimension=0,
        tiled=True,
    )
    return summed.T.astype(bf16)


def solution(mesh):
    placed = (
        P("seq", "chan"),
        P("seq", "chan"),
        P("seq", "chan"),
        P("seq", "chan"),
        P("chan"),
        P("chan", None),
    )
    return jax.shard_map(
        shards, mesh=mesh, in_specs=placed, out_specs=P("seq", "chan"), check_vma=False
    )
```

```python
import functools
import math

import jax
import jax.numpy as jnp
import numpy as np
from jax import lax
from jax.experimental import pallas as pl
from jax.experimental.pallas import tpu as pltpu
from jax.sharding import PartitionSpec as P

f32 = jnp.float32
bf16 = jnp.bfloat16


def twiddles(numerator, modulus):
    angles = 2.0 * math.pi / modulus * (numerator % modulus).astype(f32)
    return jnp.cos(angles), jnp.sin(angles)


def convolve(signal, long_filter):
    groups = lax.axis_size("seq")
    seq_len, channels = signal.shape
    padded = 2 * groups * seq_len
    own = channels // groups
    stacked = jnp.stack([long_filter, signal])
    got = lax.all_to_all(stacked, "seq", split_axis=2, concat_axis=1, tiled=True)
    blocks = got.reshape(2, groups, seq_len, own)
    classes = jnp.arange(groups + 1, dtype=jnp.int32)
    devs = jnp.arange(groups, dtype=jnp.int32)
    offsets = jnp.arange(seq_len, dtype=jnp.int32)
    cos_dev, sin_dev = twiddles(classes[:, None] * devs[None, :], 2 * groups)
    cos_tw, sin_tw = twiddles(classes[:, None] * offsets[None, :], padded)
    cos_tw, sin_tw = cos_tw[:, :, None], sin_tw[:, :, None]
    cos_seq, sin_seq = twiddles(offsets[:, None] * offsets[None, :], seq_len)
    fourier = jnp.concatenate(
        [
            jnp.concatenate([cos_seq, sin_seq], axis=1),
            jnp.concatenate([-sin_seq, cos_seq], axis=1),
        ],
        axis=0,
    ).astype(bf16)
    real = jnp.einsum("kd,sdmc->skmc", cos_dev.astype(bf16), blocks, preferred_element_type=f32)
    imag = -jnp.einsum("kd,sdmc->skmc", sin_dev.astype(bf16), blocks, preferred_element_type=f32)
    turned = jnp.concatenate(
        [real * cos_tw + imag * sin_tw, imag * cos_tw - real * sin_tw], axis=2
    ).astype(bf16)
    spectra = jnp.einsum("ab,skbc->skac", fourier, turned, preferred_element_type=f32)
    f_re, f_im = spectra[0, :, :seq_len], spectra[0, :, seq_len:]
    s_re, s_im = spectra[1, :, :seq_len], spectra[1, :, seq_len:]
    prod = jnp.concatenate(
        [f_re * s_re - f_im * s_im, -(f_re * s_im + f_im * s_re)], axis=1
    ).astype(bf16)
    back = jnp.einsum("ab,kbc->kac", fourier, prod, preferred_element_type=f32)
    b_re, b_im = back[:, :seq_len], -back[:, seq_len:]
    r_re = (b_re * cos_tw - b_im * sin_tw).astype(bf16)
    r_im = (b_re * sin_tw + b_im * cos_tw).astype(bf16)
    weight = jnp.where((classes == 0) | (classes == groups), 1.0, 2.0)[:, None]
    conv = jnp.einsum(
        "kd,kmc->dmc", (cos_dev * weight).astype(bf16), r_re, preferred_element_type=f32
    ) - jnp.einsum(
        "kd,kmc->dmc", (sin_dev * weight).astype(bf16), r_im, preferred_element_type=f32
    )
    conv = (conv * (1.0 / padded)).astype(bf16).reshape(groups * seq_len, own)
    return lax.all_to_all(conv, "seq", split_axis=0, concat_axis=1, tiled=True).astype(f32)


LANES = 128
AHEAD = 3
PARTS = (4, 4, 4, 4, 4, 4, 4, 4)


def layer_kernel(
    sizes,
    gate_hbm, key_hbm, value_hbm, filt_hbm, skip_ref, weight_hbm, forward_hbm, inverse_hbm,
    out_ref,
    gate, key, value, weight, forward, inverse,
    filt_in, sig_in, sig, filt_spec, sig_spec, prod, conv_out, conv_in, gated,
    own, pair_out, pair_in, cross_out, cross_in,
    load_sem, fsend, frecv, ssend, srecv, csend, crecv, psend, precv, xsend, xrecv,
):
    groups, rows = filt_in.shape[0], filt_in.shape[1]
    me = lax.axis_index("seq")
    chan = lax.axis_index("chan")
    core = lax.rem(chan, 2)
    side = chan // 2
    pair = chan + 1 - 2 * core
    cross = lax.rem(chan + 2, 4)
    columns = weight.shape[2]
    chunks = len(sizes)
    starts = [sum(sizes[:q]) for q in range(chunks)]
    peers = [lax.rem(me + j, groups) for j in range(groups)]
    origins = [lax.rem(me + groups - j, groups) for j in range(groups)]

    def load(src, dst, at):
        copy = pltpu.make_async_copy(src, dst, load_sem.at[at])
        copy.start()
        return copy

    def lanes_of(p):
        return pl.ds(pl.multiple_of(p * LANES, LANES), LANES)

    key_load = load(key_hbm, key, 0)
    value_load = load(value_hbm, value, 1)

    barrier = pltpu.get_barrier_semaphore()
    for j in range(1, groups):
        pl.semaphore_signal(barrier, inc=1, device_id={"seq": peers[j]}, device_id_type=pl.DeviceIdType.MESH)
    for other in (pair, cross):
        pl.semaphore_signal(barrier, inc=1, device_id={"chan": other}, device_id_type=pl.DeviceIdType.MESH)
    pl.semaphore_wait(barrier, groups + 1)

    def remote(src, dst, send, recv, where):
        copy = pltpu.make_async_remote_copy(
            src_ref=src, dst_ref=dst, send_sem=send, recv_sem=recv,
            device_id=where, device_id_type=pl.DeviceIdType.MESH,
        )
        copy.start()
        return copy

    filt_copies = [
        remote(filt_hbm.at[:, lanes_of(peers[j])], filt_in.at[me], fsend.at[j], frecv.at[j], {"seq": peers[j]})
        for j in range(1, groups)
    ]
    key_load.wait()
    value_load.wait()

    def multiply(i, _):
        at = pl.ds(i * 32, 32)
        for p in range(groups):
            cols = slice(p * LANES, (p + 1) * LANES)
            sig[p, at, :] = (key[at, cols].astype(f32) * value[at, cols].astype(f32)).astype(bf16)
        return 0

    lax.fori_loop(0, rows // 32, multiply, 0)
    sig_copies = [
        remote(sig.at[peers[j]], sig_in.at[me], ssend.at[j], srecv.at[j], {"seq": peers[j]})
        for j in range(1, groups)
    ]
    filt_own = load(filt_hbm.at[:, lanes_of(me)], filt_in.at[me], 2)
    forward_load = load(forward_hbm, forward, 3)
    late = [load(inverse_hbm, inverse, 4), load(gate_hbm, gate, 5)] + [
        load(weight_hbm.at[:, pl.ds(b * columns, columns)], weight.at[b], 6 + b) for b in range(4)
    ]
    sig_in[me] = sig[me]

    def transform(src, spec, first, second):
        def body(i, _):
            at = pl.ds(i * 256, 256)
            both = jnp.concatenate([src[first], src[second]], axis=1)
            acc = jnp.dot(forward[at, :], both, preferred_element_type=f32)
            spec[first, at, :] = acc[:, :LANES]
            spec[second, at, :] = acc[:, LANES:]
            return 0

        lax.fori_loop(0, 2 * rows // 256, body, 0)

    def transform_all(src, spec, copies):
        for j in range(0, groups, 2):
            for copy in copies[max(j - 1, 0) : j + 1]:
                copy.wait_recv()
            transform(src, spec, origins[j], origins[j + 1])

    forward_load.wait()
    filt_own.wait()
    transform_all(filt_in, filt_spec, filt_copies)
    scale = 1.0 / rows

    def overlap(i, _):
        for first, sign in ((0, 1.0), (rows // 2, -1.0)):
            at = pl.ds(first + i * 8, 8)
            low = pl.ds(rows + first + i * 8, 8)
            last_re, last_im = None, None
            for j in range(groups):
                re, im = filt_spec[j, at, :] * scale, filt_spec[j, low, :] * scale
                if j == 0:
                    filt_spec[j, at, :], filt_spec[j, low, :] = re, im
                else:
                    filt_spec[j, at, :] = re - sign * last_im
                    filt_spec[j, low, :] = im + sign * last_re
                last_re, last_im = re, im
        return 0

    lax.fori_loop(0, rows // 16, overlap, 0)
    transform_all(sig_in, sig_spec, sig_copies)

    def multiply_spectra(i, _):
        at = pl.ds(i * 16, 16)
        low = pl.ds(rows + i * 16, 16)
        for n in range(groups):
            re, im = None, None
            for j in range(n + 1):
                f_re, f_im = filt_spec[j, at, :], filt_spec[j, low, :]
                s_re, s_im = sig_spec[n - j, at, :], sig_spec[n - j, low, :]
                t_re, t_im = f_re * s_re - f_im * s_im, f_re * s_im + f_im * s_re
                re, im = (t_re, t_im) if j == 0 else (re + t_re, im + t_im)
            cols = slice(n * LANES, (n + 1) * LANES)
            prod[at, cols] = re.astype(bf16)
            prod[low, cols] = im.astype(bf16)
        return 0

    lax.fori_loop(0, rows // 16, multiply_spectra, 0)
    for copy in late:
        copy.wait()

    conv_copies = []

    def send_conv(q):
        span = pl.ds(starts[q], sizes[q])
        back = jnp.dot(inverse[span, :], prod[...], preferred_element_type=f32)
        for d in range(groups):
            conv_out[d, span, :] = back[:, d * LANES : (d + 1) * LANES].astype(bf16)
        conv_copies.append(
            [
                remote(
                    conv_out.at[peers[j], span], conv_in.at[me, span],
                    csend.at[q, j], crecv.at[q, j], {"seq": peers[j]},
                )
                for j in range(1, groups)
            ]
        )
        conv_in[me, span, :] = conv_out[me, span, :]

    for q in range(min(AHEAD, chunks)):
        send_conv(q)

    pair_copies, cross_copies = [], []
    there, here = 1 - side, side

    def project(q, x, is_pair):
        chunk, span = sizes[q], pl.ds(starts[q], sizes[q])
        part = jnp.dot(
            gated[:chunk, :],
            weight[2 * x + (1 - core if is_pair else core)],
            preferred_element_type=f32,
        )
        if not is_pair:
            own[x, span, :] = part
            return
        pair_out[x, span, :] = part.astype(bf16)
        at = 2 * q + (0 if x is there else 1)
        pair_copies.append(
            remote(
                pair_out.at[x, span], pair_in.at[x, span],
                psend.at[at], precv.at[at], {"chan": pair},
            )
        )

    def finish(q):
        span = pl.ds(starts[q], sizes[q])
        cross_copies[q].wait_recv()
        out_ref[span, :] = (own[here, span, :] + cross_in[span, :].astype(f32)).astype(bf16)

    for q in range(chunks):
        for copy in conv_copies[q]:
            copy.wait_recv()
        chunk = sizes[q]
        rows_q = slice(starts[q], starts[q] + chunk)
        span = pl.ds(starts[q], chunk)
        for s in range(groups):
            cols = slice(s * LANES, (s + 1) * LANES)
            mixed = conv_in[s, rows_q, :].astype(f32) + skip_ref[:, cols] * sig[s, rows_q, :].astype(f32)
            gated[:chunk, cols] = (gate[rows_q, cols].astype(f32) * mixed).astype(bf16)
        project(q, there, True)
        project(q, there, False)
        project(q, here, True)
        pair_copies[2 * q].wait_recv()
        cross_out[span, :] = (own[there, span, :] + pair_in[there, span, :].astype(f32)).astype(bf16)
        cross_copies.append(
            remote(cross_out.at[span], cross_in.at[span], xsend.at[q], xrecv.at[q], {"chan": cross})
        )
        project(q, here, False)
        if q + AHEAD < chunks:
            send_conv(q + AHEAD)
        pair_copies[2 * q + 1].wait_recv()
        own[here, span, :] = own[here, span, :] + pair_in[here, span, :].astype(f32)
        if q >= 2:
            finish(q - 2)
    for q in range(max(chunks - 2, 0), chunks):
        finish(q)

    for copy in filt_copies + sig_copies + pair_copies + cross_copies:
        copy.wait_send()
    for copies in conv_copies:
        for copy in copies:
            copy.wait_send()


def transform_matrices(rows):
    freq = np.concatenate([np.arange(0, rows, 2), np.arange(1, rows, 2)])
    numerator = ((2 * freq[:, None] + 1) * np.arange(rows)[None, :]) % (4 * rows)
    angle = np.pi / (2 * rows) * numerator
    forward = np.concatenate([np.cos(angle), -np.sin(angle)], axis=0)
    return forward.astype(jnp.bfloat16), np.ascontiguousarray(forward.T).astype(jnp.bfloat16)


def fused(gate_query, key_input, value_input, long_filter, skip_gain, out_weight, sizes):
    groups = lax.axis_size("seq")
    rows, channels = gate_query.shape
    columns = out_weight.shape[1] // 4
    chunks, chunk = len(sizes), max(sizes)
    forward, inverse = transform_matrices(rows)
    blocks = (groups, rows, LANES)
    spectra = (groups, 2 * rows, LANES)
    dma = pltpu.SemaphoreType.DMA
    anywhere = pl.BlockSpec(memory_space=pl.ANY)
    in_vmem = pl.BlockSpec(memory_space=pltpu.VMEM)
    return pl.pallas_call(
        functools.partial(layer_kernel, sizes),
        out_shape=pltpu.VMEM((rows, columns), bf16),
        in_specs=[anywhere] * 4 + [in_vmem] + [anywhere] * 3,
        out_specs=in_vmem,
        scratch_shapes=[
            pltpu.VMEM((rows, channels), bf16),
            pltpu.VMEM((rows, channels), bf16),
            pltpu.VMEM((rows, channels), bf16),
            pltpu.VMEM((4, channels, columns), bf16),
            pltpu.VMEM((2 * rows, rows), bf16),
            pltpu.VMEM((rows, 2 * rows), bf16),
            pltpu.VMEM(blocks, bf16),
            pltpu.VMEM(blocks, bf16),
            pltpu.VMEM(blocks, bf16),
            pltpu.VMEM(spectra, f32),
            pltpu.VMEM(spectra, f32),
            pltpu.VMEM((2 * rows, groups * LANES), bf16),
            pltpu.VMEM(blocks, bf16),
            pltpu.VMEM(blocks, bf16),
            pltpu.VMEM((chunk, channels), bf16),
            pltpu.VMEM((2, rows, columns), f32),
            pltpu.VMEM((2, rows, columns), bf16),
            pltpu.VMEM((2, rows, columns), bf16),
            pltpu.VMEM((rows, columns), bf16),
            pltpu.VMEM((rows, columns), bf16),
            dma((10,)),
            dma((groups,)),
            dma((groups,)),
            dma((groups,)),
            dma((groups,)),
            dma((chunks, groups)),
            dma((chunks, groups)),
            dma((2 * chunks,)),
            dma((2 * chunks,)),
            dma((chunks,)),
            dma((chunks,)),
        ],
        compiler_params=pltpu.CompilerParams(
            collective_id=0, has_side_effects=True, vmem_limit_bytes=56 * 1024 * 1024
        ),
        name="layer",
    )(
        gate_query, key_input, value_input, long_filter, skip_gain[None, :], out_weight,
        jnp.asarray(forward), jnp.asarray(inverse),
    )


def chunk_sizes(rows):
    return tuple(rows * part // sum(PARTS) for part in PARTS)


def groups_fit(block, weight, chans):
    rows, channels = block
    return (
        lax.axis_size("seq") == 8
        and chans == 4
        and channels == 8 * LANES
        and rows % 256 == 0
        and rows <= 512
        and weight[1] % (4 * LANES) == 0
        and weight[1] <= 4096
    )


def shards(gate_query, key_input, value_input, long_filter, skip_gain, out_weight):
    chans = lax.axis_size("chan")
    if groups_fit(gate_query.shape, out_weight.shape, chans):
        return fused(
            gate_query, key_input, value_input, long_filter, skip_gain, out_weight, chunk_sizes(gate_query.shape[0])
        )
    signal = (key_input.astype(f32) * value_input.astype(f32)).astype(bf16)
    conv = convolve(signal, long_filter)
    gated = (
        gate_query.astype(f32) * (conv + skip_gain[None, :] * signal.astype(f32))
    ).astype(bf16)
    summed = lax.psum_scatter(
        lax.dot_general(
            out_weight, gated, (((0,), (1,)), ((), ())), preferred_element_type=f32
        ).astype(bf16),
        "chan",
        scatter_dimension=0,
        tiled=True,
    )
    return summed.T.astype(bf16)


def solution(mesh):
    placed = (
        P("seq", "chan"),
        P("seq", "chan"),
        P("seq", "chan"),
        P("seq", "chan"),
        P("chan"),
        P("chan", None),
    )
    return jax.shard_map(
        shards, mesh=mesh, in_specs=placed, out_specs=P("seq", "chan"), check_vma=False
    )
```

```python
import functools
import math

import jax
import jax.numpy as jnp
import numpy as np
from jax import lax
from jax.experimental import pallas as pl
from jax.experimental.pallas import tpu as pltpu
from jax.sharding import PartitionSpec as P

f32 = jnp.float32
bf16 = jnp.bfloat16


def twiddles(numerator, modulus):
    angles = 2.0 * math.pi / modulus * (numerator % modulus).astype(f32)
    return jnp.cos(angles), jnp.sin(angles)


def convolve(signal, long_filter):
    groups = lax.axis_size("seq")
    seq_len, channels = signal.shape
    padded = 2 * groups * seq_len
    own = channels // groups
    stacked = jnp.stack([long_filter, signal])
    got = lax.all_to_all(stacked, "seq", split_axis=2, concat_axis=1, tiled=True)
    blocks = got.reshape(2, groups, seq_len, own)
    classes = jnp.arange(groups + 1, dtype=jnp.int32)
    devs = jnp.arange(groups, dtype=jnp.int32)
    offsets = jnp.arange(seq_len, dtype=jnp.int32)
    cos_dev, sin_dev = twiddles(classes[:, None] * devs[None, :], 2 * groups)
    cos_tw, sin_tw = twiddles(classes[:, None] * offsets[None, :], padded)
    cos_tw, sin_tw = cos_tw[:, :, None], sin_tw[:, :, None]
    cos_seq, sin_seq = twiddles(offsets[:, None] * offsets[None, :], seq_len)
    fourier = jnp.concatenate(
        [
            jnp.concatenate([cos_seq, sin_seq], axis=1),
            jnp.concatenate([-sin_seq, cos_seq], axis=1),
        ],
        axis=0,
    ).astype(bf16)
    real = jnp.einsum("kd,sdmc->skmc", cos_dev.astype(bf16), blocks, preferred_element_type=f32)
    imag = -jnp.einsum("kd,sdmc->skmc", sin_dev.astype(bf16), blocks, preferred_element_type=f32)
    turned = jnp.concatenate(
        [real * cos_tw + imag * sin_tw, imag * cos_tw - real * sin_tw], axis=2
    ).astype(bf16)
    spectra = jnp.einsum("ab,skbc->skac", fourier, turned, preferred_element_type=f32)
    f_re, f_im = spectra[0, :, :seq_len], spectra[0, :, seq_len:]
    s_re, s_im = spectra[1, :, :seq_len], spectra[1, :, seq_len:]
    prod = jnp.concatenate(
        [f_re * s_re - f_im * s_im, -(f_re * s_im + f_im * s_re)], axis=1
    ).astype(bf16)
    back = jnp.einsum("ab,kbc->kac", fourier, prod, preferred_element_type=f32)
    b_re, b_im = back[:, :seq_len], -back[:, seq_len:]
    r_re = (b_re * cos_tw - b_im * sin_tw).astype(bf16)
    r_im = (b_re * sin_tw + b_im * cos_tw).astype(bf16)
    weight = jnp.where((classes == 0) | (classes == groups), 1.0, 2.0)[:, None]
    conv = jnp.einsum(
        "kd,kmc->dmc", (cos_dev * weight).astype(bf16), r_re, preferred_element_type=f32
    ) - jnp.einsum(
        "kd,kmc->dmc", (sin_dev * weight).astype(bf16), r_im, preferred_element_type=f32
    )
    conv = (conv * (1.0 / padded)).astype(bf16).reshape(groups * seq_len, own)
    return lax.all_to_all(conv, "seq", split_axis=0, concat_axis=1, tiled=True).astype(f32)


LANES = 128
AHEAD = 3
PARTS = (4, 4, 4, 4, 4, 4, 4, 4)


def layer_kernel(
    sizes,
    gate_hbm, key_hbm, value_hbm, filt_hbm, skip_ref, weight_hbm, forward_hbm, inverse_hbm,
    out_ref,
    gate, key, value, weight, forward, inverse,
    filt_in, sig_in, sig, filt_spec, sig_spec, prod, conv_out, conv_in, gated,
    own, pair_out, pair_in, cross_out, cross_in,
    load_sem, fsend, frecv, ssend, srecv, csend, crecv, psend, precv, xsend, xrecv,
):
    groups, rows = filt_in.shape[0], filt_in.shape[1]
    me = lax.axis_index("seq")
    chan = lax.axis_index("chan")
    core = lax.rem(chan, 2)
    side = chan // 2
    pair = chan + 1 - 2 * core
    cross = lax.rem(chan + 2, 4)
    columns = weight.shape[2]
    chunks = len(sizes)
    starts = [sum(sizes[:q]) for q in range(chunks)]
    near = groups // 2
    half, at_half = me // near, lax.rem(me, near)
    steps = [lax.rem(at_half + i, near) for i in range(near)]
    back_steps = [lax.rem(at_half + near - i, near) for i in range(near)]
    first_near, first_far = half * near, (1 - half) * near
    peers = [first_near + i for i in steps] + [first_far + i for i in steps]
    origins = [first_near + i for i in back_steps] + [first_far + i for i in back_steps]

    def load(src, dst, at):
        copy = pltpu.make_async_copy(src, dst, load_sem.at[at])
        copy.start()
        return copy

    def lanes_of(p):
        return pl.ds(pl.multiple_of(p * LANES, LANES), LANES)

    key_load = load(key_hbm, key, 0)
    value_load = load(value_hbm, value, 1)

    barrier = pltpu.get_barrier_semaphore()
    for j in range(1, groups):
        pl.semaphore_signal(barrier, inc=1, device_id={"seq": peers[j]}, device_id_type=pl.DeviceIdType.MESH)
    for other in (pair, cross):
        pl.semaphore_signal(barrier, inc=1, device_id={"chan": other}, device_id_type=pl.DeviceIdType.MESH)
    pl.semaphore_wait(barrier, groups + 1)

    def remote(src, dst, send, recv, where):
        copy = pltpu.make_async_remote_copy(
            src_ref=src, dst_ref=dst, send_sem=send, recv_sem=recv,
            device_id=where, device_id_type=pl.DeviceIdType.MESH,
        )
        copy.start()
        return copy

    filt_copies = [
        remote(filt_hbm.at[:, lanes_of(peers[j])], filt_in.at[me], fsend.at[j], frecv.at[j], {"seq": peers[j]})
        for j in range(1, groups)
    ]
    key_load.wait()
    value_load.wait()

    def multiply(i, _):
        at = pl.ds(i * 32, 32)
        for p in range(groups):
            cols = slice(p * LANES, (p + 1) * LANES)
            sig[p, at, :] = (key[at, cols].astype(f32) * value[at, cols].astype(f32)).astype(bf16)
        return 0

    lax.fori_loop(0, rows // 32, multiply, 0)
    sig_copies = [
        remote(sig.at[peers[j]], sig_in.at[me], ssend.at[j], srecv.at[j], {"seq": peers[j]})
        for j in range(1, groups)
    ]
    filt_own = load(filt_hbm.at[:, lanes_of(me)], filt_in.at[me], 2)
    forward_load = load(forward_hbm, forward, 3)
    late = [load(inverse_hbm, inverse, 4), load(gate_hbm, gate, 5)] + [
        load(weight_hbm.at[:, pl.ds(b * columns, columns)], weight.at[b], 6 + b) for b in range(4)
    ]
    sig_in[me] = sig[me]

    def transform(src, spec, first, second):
        def body(i, _):
            at = pl.ds(i * 256, 256)
            both = jnp.concatenate([src[first], src[second]], axis=1)
            acc = jnp.dot(forward[at, :], both, preferred_element_type=f32)
            spec[first, at, :] = acc[:, :LANES]
            spec[second, at, :] = acc[:, LANES:]
            return 0

        lax.fori_loop(0, 2 * rows // 256, body, 0)

    def transform_all(src, spec, copies):
        for j in range(0, groups, 2):
            for copy in copies[max(j - 1, 0) : j + 1]:
                copy.wait_recv()
            transform(src, spec, origins[j], origins[j + 1])

    forward_load.wait()
    filt_own.wait()
    transform_all(filt_in, filt_spec, filt_copies)
    scale = 1.0 / rows

    def overlap(i, _):
        for first, sign in ((0, 1.0), (rows // 2, -1.0)):
            at = pl.ds(first + i * 8, 8)
            low = pl.ds(rows + first + i * 8, 8)
            last_re, last_im = None, None
            for j in range(groups):
                re, im = filt_spec[j, at, :] * scale, filt_spec[j, low, :] * scale
                if j == 0:
                    filt_spec[j, at, :], filt_spec[j, low, :] = re, im
                else:
                    filt_spec[j, at, :] = re - sign * last_im
                    filt_spec[j, low, :] = im + sign * last_re
                last_re, last_im = re, im
        return 0

    lax.fori_loop(0, rows // 16, overlap, 0)
    transform_all(sig_in, sig_spec, sig_copies)

    def multiply_spectra(i, _):
        at = pl.ds(i * 16, 16)
        low = pl.ds(rows + i * 16, 16)
        for n in range(groups):
            re, im = None, None
            for j in range(n + 1):
                f_re, f_im = filt_spec[j, at, :], filt_spec[j, low, :]
                s_re, s_im = sig_spec[n - j, at, :], sig_spec[n - j, low, :]
                t_re, t_im = f_re * s_re - f_im * s_im, f_re * s_im + f_im * s_re
                re, im = (t_re, t_im) if j == 0 else (re + t_re, im + t_im)
            cols = slice(n * LANES, (n + 1) * LANES)
            prod[at, cols] = re.astype(bf16)
            prod[low, cols] = im.astype(bf16)
        return 0

    lax.fori_loop(0, rows // 16, multiply_spectra, 0)
    for copy in late:
        copy.wait()

    conv_copies = []

    def send_conv(q):
        span = pl.ds(starts[q], sizes[q])
        back = jnp.dot(inverse[span, :], prod[...], preferred_element_type=f32)
        for d in range(groups):
            conv_out[d, span, :] = back[:, d * LANES : (d + 1) * LANES].astype(bf16)
        conv_copies.append(
            [
                remote(
                    conv_out.at[peers[j], span], conv_in.at[me, span],
                    csend.at[q, j], crecv.at[q, j], {"seq": peers[j]},
                )
                for j in range(1, groups)
            ]
        )
        conv_in[me, span, :] = conv_out[me, span, :]

    for q in range(min(AHEAD, chunks)):
        send_conv(q)

    pair_copies, cross_copies = [], []
    there, here = 1 - side, side

    def project(q, x, is_pair):
        chunk, span = sizes[q], pl.ds(starts[q], sizes[q])
        part = jnp.dot(
            gated[:chunk, :],
            weight[2 * x + (1 - core if is_pair else core)],
            preferred_element_type=f32,
        )
        if not is_pair:
            own[x, span, :] = part
            return
        pair_out[x, span, :] = part.astype(bf16)
        at = 2 * q + (0 if x is there else 1)
        pair_copies.append(
            remote(
                pair_out.at[x, span], pair_in.at[x, span],
                psend.at[at], precv.at[at], {"chan": pair},
            )
        )

    def finish(q):
        span = pl.ds(starts[q], sizes[q])
        cross_copies[q].wait_recv()
        out_ref[span, :] = (own[here, span, :] + cross_in[span, :].astype(f32)).astype(bf16)

    for q in range(chunks):
        for copy in conv_copies[q]:
            copy.wait_recv()
        chunk = sizes[q]
        rows_q = slice(starts[q], starts[q] + chunk)
        span = pl.ds(starts[q], chunk)
        for s in range(groups):
            cols = slice(s * LANES, (s + 1) * LANES)
            mixed = conv_in[s, rows_q, :].astype(f32) + skip_ref[:, cols] * sig[s, rows_q, :].astype(f32)
            gated[:chunk, cols] = (gate[rows_q, cols].astype(f32) * mixed).astype(bf16)
        project(q, there, True)
        project(q, there, False)
        project(q, here, True)
        pair_copies[2 * q].wait_recv()
        cross_out[span, :] = (own[there, span, :] + pair_in[there, span, :].astype(f32)).astype(bf16)
        cross_copies.append(
            remote(cross_out.at[span], cross_in.at[span], xsend.at[q], xrecv.at[q], {"chan": cross})
        )
        project(q, here, False)
        if q + AHEAD < chunks:
            send_conv(q + AHEAD)
        pair_copies[2 * q + 1].wait_recv()
        own[here, span, :] = own[here, span, :] + pair_in[here, span, :].astype(f32)
        if q >= 2:
            finish(q - 2)
    for q in range(max(chunks - 2, 0), chunks):
        finish(q)

    for copy in filt_copies + sig_copies + pair_copies + cross_copies:
        copy.wait_send()
    for copies in conv_copies:
        for copy in copies:
            copy.wait_send()


def transform_matrices(rows):
    freq = np.concatenate([np.arange(0, rows, 2), np.arange(1, rows, 2)])
    numerator = ((2 * freq[:, None] + 1) * np.arange(rows)[None, :]) % (4 * rows)
    angle = np.pi / (2 * rows) * numerator
    forward = np.concatenate([np.cos(angle), -np.sin(angle)], axis=0)
    return forward.astype(jnp.bfloat16), np.ascontiguousarray(forward.T).astype(jnp.bfloat16)


def fused(gate_query, key_input, value_input, long_filter, skip_gain, out_weight, sizes):
    groups = lax.axis_size("seq")
    rows, channels = gate_query.shape
    columns = out_weight.shape[1] // 4
    chunks, chunk = len(sizes), max(sizes)
    forward, inverse = transform_matrices(rows)
    blocks = (groups, rows, LANES)
    spectra = (groups, 2 * rows, LANES)
    dma = pltpu.SemaphoreType.DMA
    anywhere = pl.BlockSpec(memory_space=pl.ANY)
    in_vmem = pl.BlockSpec(memory_space=pltpu.VMEM)
    return pl.pallas_call(
        functools.partial(layer_kernel, sizes),
        out_shape=pltpu.VMEM((rows, columns), bf16),
        in_specs=[anywhere] * 4 + [in_vmem] + [anywhere] * 3,
        out_specs=in_vmem,
        scratch_shapes=[
            pltpu.VMEM((rows, channels), bf16),
            pltpu.VMEM((rows, channels), bf16),
            pltpu.VMEM((rows, channels), bf16),
            pltpu.VMEM((4, channels, columns), bf16),
            pltpu.VMEM((2 * rows, rows), bf16),
            pltpu.VMEM((rows, 2 * rows), bf16),
            pltpu.VMEM(blocks, bf16),
            pltpu.VMEM(blocks, bf16),
            pltpu.VMEM(blocks, bf16),
            pltpu.VMEM(spectra, f32),
            pltpu.VMEM(spectra, f32),
            pltpu.VMEM((2 * rows, groups * LANES), bf16),
            pltpu.VMEM(blocks, bf16),
            pltpu.VMEM(blocks, bf16),
            pltpu.VMEM((chunk, channels), bf16),
            pltpu.VMEM((2, rows, columns), f32),
            pltpu.VMEM((2, rows, columns), bf16),
            pltpu.VMEM((2, rows, columns), bf16),
            pltpu.VMEM((rows, columns), bf16),
            pltpu.VMEM((rows, columns), bf16),
            dma((10,)),
            dma((groups,)),
            dma((groups,)),
            dma((groups,)),
            dma((groups,)),
            dma((chunks, groups)),
            dma((chunks, groups)),
            dma((2 * chunks,)),
            dma((2 * chunks,)),
            dma((chunks,)),
            dma((chunks,)),
        ],
        compiler_params=pltpu.CompilerParams(
            collective_id=0, has_side_effects=True, vmem_limit_bytes=56 * 1024 * 1024
        ),
        name="layer",
    )(
        gate_query, key_input, value_input, long_filter, skip_gain[None, :], out_weight,
        jnp.asarray(forward), jnp.asarray(inverse),
    )


def chunk_sizes(rows):
    return tuple(rows * part // sum(PARTS) for part in PARTS)


def groups_fit(block, weight, chans):
    rows, channels = block
    return (
        lax.axis_size("seq") == 8
        and chans == 4
        and channels == 8 * LANES
        and rows % 256 == 0
        and rows <= 512
        and weight[1] % (4 * LANES) == 0
        and weight[1] <= 4096
    )


def shards(gate_query, key_input, value_input, long_filter, skip_gain, out_weight):
    chans = lax.axis_size("chan")
    if groups_fit(gate_query.shape, out_weight.shape, chans):
        return fused(
            gate_query, key_input, value_input, long_filter, skip_gain, out_weight, chunk_sizes(gate_query.shape[0])
        )
    signal = (key_input.astype(f32) * value_input.astype(f32)).astype(bf16)
    conv = convolve(signal, long_filter)
    gated = (
        gate_query.astype(f32) * (conv + skip_gain[None, :] * signal.astype(f32))
    ).astype(bf16)
    summed = lax.psum_scatter(
        lax.dot_general(
            out_weight, gated, (((0,), (1,)), ((), ())), preferred_element_type=f32
        ).astype(bf16),
        "chan",
        scatter_dimension=0,
        tiled=True,
    )
    return summed.T.astype(bf16)


def solution(mesh):
    placed = (
        P("seq", "chan"),
        P("seq", "chan"),
        P("seq", "chan"),
        P("seq", "chan"),
        P("chan"),
        P("chan", None),
    )
    return jax.shard_map(
        shards, mesh=mesh, in_specs=placed, out_specs=P("seq", "chan"), check_vma=False
    )
```

```python
import functools
import math

import jax
import jax.numpy as jnp
import numpy as np
from jax import lax
from jax.experimental import pallas as pl
from jax.experimental.pallas import tpu as pltpu
from jax.sharding import PartitionSpec as P

f32 = jnp.float32
bf16 = jnp.bfloat16


def twiddles(numerator, modulus):
    angles = 2.0 * math.pi / modulus * (numerator % modulus).astype(f32)
    return jnp.cos(angles), jnp.sin(angles)


def convolve(signal, long_filter):
    groups = lax.axis_size("seq")
    seq_len, channels = signal.shape
    padded = 2 * groups * seq_len
    own = channels // groups
    stacked = jnp.stack([long_filter, signal])
    got = lax.all_to_all(stacked, "seq", split_axis=2, concat_axis=1, tiled=True)
    blocks = got.reshape(2, groups, seq_len, own)
    classes = jnp.arange(groups + 1, dtype=jnp.int32)
    devs = jnp.arange(groups, dtype=jnp.int32)
    offsets = jnp.arange(seq_len, dtype=jnp.int32)
    cos_dev, sin_dev = twiddles(classes[:, None] * devs[None, :], 2 * groups)
    cos_tw, sin_tw = twiddles(classes[:, None] * offsets[None, :], padded)
    cos_tw, sin_tw = cos_tw[:, :, None], sin_tw[:, :, None]
    cos_seq, sin_seq = twiddles(offsets[:, None] * offsets[None, :], seq_len)
    fourier = jnp.concatenate(
        [
            jnp.concatenate([cos_seq, sin_seq], axis=1),
            jnp.concatenate([-sin_seq, cos_seq], axis=1),
        ],
        axis=0,
    ).astype(bf16)
    real = jnp.einsum("kd,sdmc->skmc", cos_dev.astype(bf16), blocks, preferred_element_type=f32)
    imag = -jnp.einsum("kd,sdmc->skmc", sin_dev.astype(bf16), blocks, preferred_element_type=f32)
    turned = jnp.concatenate(
        [real * cos_tw + imag * sin_tw, imag * cos_tw - real * sin_tw], axis=2
    ).astype(bf16)
    spectra = jnp.einsum("ab,skbc->skac", fourier, turned, preferred_element_type=f32)
    f_re, f_im = spectra[0, :, :seq_len], spectra[0, :, seq_len:]
    s_re, s_im = spectra[1, :, :seq_len], spectra[1, :, seq_len:]
    prod = jnp.concatenate(
        [f_re * s_re - f_im * s_im, -(f_re * s_im + f_im * s_re)], axis=1
    ).astype(bf16)
    back = jnp.einsum("ab,kbc->kac", fourier, prod, preferred_element_type=f32)
    b_re, b_im = back[:, :seq_len], -back[:, seq_len:]
    r_re = (b_re * cos_tw - b_im * sin_tw).astype(bf16)
    r_im = (b_re * sin_tw + b_im * cos_tw).astype(bf16)
    weight = jnp.where((classes == 0) | (classes == groups), 1.0, 2.0)[:, None]
    conv = jnp.einsum(
        "kd,kmc->dmc", (cos_dev * weight).astype(bf16), r_re, preferred_element_type=f32
    ) - jnp.einsum(
        "kd,kmc->dmc", (sin_dev * weight).astype(bf16), r_im, preferred_element_type=f32
    )
    conv = (conv * (1.0 / padded)).astype(bf16).reshape(groups * seq_len, own)
    return lax.all_to_all(conv, "seq", split_axis=0, concat_axis=1, tiled=True).astype(f32)


LANES = 128
AHEAD = 3
PARTS = (4, 4, 4, 4, 4, 4, 4, 4)


def layer_kernel(
    sizes,
    gate_hbm, key_hbm, value_hbm, filt_hbm, skip_ref, weight_hbm, forward_hbm, inverse_hbm,
    out_ref,
    gate, key, value, weight, forward, inverse,
    filt_in, sig_in, sig, filt_spec, sig_spec, prod, conv_out, conv_in, gated,
    own, pair_out, pair_in, cross_out, cross_in,
    load_sem, fsend, frecv, ssend, srecv, csend, crecv, psend, precv, xsend, xrecv,
):
    groups, rows = filt_in.shape[0], filt_in.shape[1]
    me = lax.axis_index("seq")
    chan = lax.axis_index("chan")
    core = lax.rem(chan, 2)
    side = chan // 2
    pair = chan + 1 - 2 * core
    cross = lax.rem(chan + 2, 4)
    columns = weight.shape[2]
    chunks = len(sizes)
    starts = [sum(sizes[:q]) for q in range(chunks)]
    near = groups // 2
    half, at_half = me // near, lax.rem(me, near)
    steps = [lax.rem(at_half + i, near) for i in range(near)]
    back_steps = [lax.rem(at_half + near - i, near) for i in range(near)]
    first_near, first_far = half * near, (1 - half) * near
    peers = [first_near + i for i in steps] + [first_far + i for i in steps]
    origins = [first_near + i for i in back_steps] + [first_far + i for i in back_steps]

    def load(src, dst, at):
        copy = pltpu.make_async_copy(src, dst, load_sem.at[at])
        copy.start()
        return copy

    def lanes_of(p):
        return pl.ds(pl.multiple_of(p * LANES, LANES), LANES)

    key_load = load(key_hbm, key, 0)
    value_load = load(value_hbm, value, 1)

    barrier = pltpu.get_barrier_semaphore()
    for j in range(1, groups):
        pl.semaphore_signal(barrier, inc=1, device_id={"seq": peers[j]}, device_id_type=pl.DeviceIdType.MESH)
    for other in (pair, cross):
        pl.semaphore_signal(barrier, inc=1, device_id={"chan": other}, device_id_type=pl.DeviceIdType.MESH)
    pl.semaphore_wait(barrier, groups + 1)

    def remote(src, dst, send, recv, where):
        copy = pltpu.make_async_remote_copy(
            src_ref=src, dst_ref=dst, send_sem=send, recv_sem=recv,
            device_id=where, device_id_type=pl.DeviceIdType.MESH,
        )
        copy.start()
        return copy

    filt_copies = [
        remote(filt_hbm.at[:, lanes_of(peers[j])], filt_in.at[me], fsend.at[j], frecv.at[j], {"seq": peers[j]})
        for j in range(1, groups)
    ]
    key_load.wait()
    value_load.wait()

    def multiply(i, _):
        at = pl.ds(i * 32, 32)
        for p in range(groups):
            cols = slice(p * LANES, (p + 1) * LANES)
            sig[p, at, :] = (key[at, cols].astype(f32) * value[at, cols].astype(f32)).astype(bf16)
        return 0

    lax.fori_loop(0, rows // 32, multiply, 0)
    sig_copies = [
        remote(sig.at[peers[j]], sig_in.at[me], ssend.at[j], srecv.at[j], {"seq": peers[j]})
        for j in range(1, groups)
    ]
    filt_own = load(filt_hbm.at[:, lanes_of(me)], filt_in.at[me], 2)
    forward_load = load(forward_hbm, forward, 3)
    late = [load(inverse_hbm, inverse, 4), load(gate_hbm, gate, 5)] + [
        load(weight_hbm.at[:, pl.ds(b * columns, columns)], weight.at[b], 6 + b) for b in range(4)
    ]
    sig_in[me] = sig[me]

    def transform(src, spec, first, second):
        def body(i, _):
            at = pl.ds(i * 256, 256)
            both = jnp.concatenate([src[first], src[second]], axis=1)
            acc = jnp.dot(forward[at, :], both, preferred_element_type=f32)
            spec[first, at, :] = acc[:, :LANES]
            spec[second, at, :] = acc[:, LANES:]
            return 0

        lax.fori_loop(0, 2 * rows // 256, body, 0)

    def transform_all(src, spec, copies):
        for j in range(0, groups, 2):
            for copy in copies[max(j - 1, 0) : j + 1]:
                copy.wait_recv()
            transform(src, spec, origins[j], origins[j + 1])

    forward_load.wait()
    filt_own.wait()
    transform_all(filt_in, filt_spec, filt_copies)
    scale = 1.0 / rows

    def overlap(i, _):
        for first, sign in ((0, 1.0), (rows // 2, -1.0)):
            at = pl.ds(first + i * 8, 8)
            low = pl.ds(rows + first + i * 8, 8)
            last_re, last_im = None, None
            for j in range(groups):
                re, im = filt_spec[j, at, :] * scale, filt_spec[j, low, :] * scale
                if j == 0:
                    filt_spec[j, at, :], filt_spec[j, low, :] = re, im
                else:
                    filt_spec[j, at, :] = re - sign * last_im
                    filt_spec[j, low, :] = im + sign * last_re
                last_re, last_im = re, im
        return 0

    lax.fori_loop(0, rows // 16, overlap, 0)
    transform_all(sig_in, sig_spec, sig_copies)

    def multiply_spectra(i, _):
        at = pl.ds(i * 16, 16)
        low = pl.ds(rows + i * 16, 16)
        for n in range(groups):
            re, im = None, None
            for j in range(n + 1):
                f_re, f_im = filt_spec[j, at, :], filt_spec[j, low, :]
                s_re, s_im = sig_spec[n - j, at, :], sig_spec[n - j, low, :]
                t_re, t_im = f_re * s_re - f_im * s_im, f_re * s_im + f_im * s_re
                re, im = (t_re, t_im) if j == 0 else (re + t_re, im + t_im)
            cols = slice(n * LANES, (n + 1) * LANES)
            prod[at, cols] = re.astype(bf16)
            prod[low, cols] = im.astype(bf16)
        return 0

    lax.fori_loop(0, rows // 16, multiply_spectra, 0)
    for copy in late:
        copy.wait()

    conv_copies = []

    def send_conv(q):
        span = pl.ds(starts[q], sizes[q])
        back = jnp.dot(inverse[span, :], prod[...], preferred_element_type=f32)
        for d in range(groups):
            conv_out[d, span, :] = back[:, d * LANES : (d + 1) * LANES].astype(bf16)
        conv_copies.append(
            [
                remote(
                    conv_out.at[peers[j], span], conv_in.at[me, span],
                    csend.at[q, j], crecv.at[q, j], {"seq": peers[j]},
                )
                for j in range(1, groups)
            ]
        )
        conv_in[me, span, :] = conv_out[me, span, :]

    for q in range(min(AHEAD, chunks)):
        send_conv(q)

    pair_copies, cross_copies = [], []
    there, here = 1 - side, side

    def project(q, x, is_pair):
        chunk, span = sizes[q], pl.ds(starts[q], sizes[q])
        part = jnp.dot(
            gated[:chunk, :],
            weight[2 * x + (1 - core if is_pair else core)],
            preferred_element_type=f32,
        )
        if not is_pair:
            own[x, span, :] = part
            return
        pair_out[x, span, :] = part.astype(bf16)
        at = 2 * q + (0 if x is there else 1)
        pair_copies.append(
            remote(
                pair_out.at[x, span], pair_in.at[x, span],
                psend.at[at], precv.at[at], {"chan": pair},
            )
        )

    def finish(q):
        span = pl.ds(starts[q], sizes[q])
        cross_copies[q].wait_recv()
        out_ref[span, :] = (own[here, span, :] + cross_in[span, :].astype(f32)).astype(bf16)

    for q in range(chunks):
        for copy in conv_copies[q]:
            copy.wait_recv()
        chunk = sizes[q]
        rows_q = slice(starts[q], starts[q] + chunk)
        span = pl.ds(starts[q], chunk)
        for s in range(groups):
            cols = slice(s * LANES, (s + 1) * LANES)
            mixed = conv_in[s, rows_q, :].astype(f32) + skip_ref[:, cols] * sig[s, rows_q, :].astype(f32)
            gated[:chunk, cols] = (gate[rows_q, cols].astype(f32) * mixed).astype(bf16)
        project(q, there, True)
        project(q, here, True)
        project(q, there, False)
        pair_copies[2 * q].wait_recv()
        cross_out[span, :] = (own[there, span, :] + pair_in[there, span, :].astype(f32)).astype(bf16)
        cross_copies.append(
            remote(cross_out.at[span], cross_in.at[span], xsend.at[q], xrecv.at[q], {"chan": cross})
        )
        project(q, here, False)
        if q + AHEAD < chunks:
            send_conv(q + AHEAD)
        pair_copies[2 * q + 1].wait_recv()
        own[here, span, :] = own[here, span, :] + pair_in[here, span, :].astype(f32)
        if q >= 2:
            finish(q - 2)
    for q in range(max(chunks - 2, 0), chunks):
        finish(q)

    for copy in filt_copies + sig_copies + pair_copies + cross_copies:
        copy.wait_send()
    for copies in conv_copies:
        for copy in copies:
            copy.wait_send()


def transform_matrices(rows):
    freq = np.concatenate([np.arange(0, rows, 2), np.arange(1, rows, 2)])
    numerator = ((2 * freq[:, None] + 1) * np.arange(rows)[None, :]) % (4 * rows)
    angle = np.pi / (2 * rows) * numerator
    forward = np.concatenate([np.cos(angle), -np.sin(angle)], axis=0)
    return forward.astype(jnp.bfloat16), np.ascontiguousarray(forward.T).astype(jnp.bfloat16)


def fused(gate_query, key_input, value_input, long_filter, skip_gain, out_weight, sizes):
    groups = lax.axis_size("seq")
    rows, channels = gate_query.shape
    columns = out_weight.shape[1] // 4
    chunks, chunk = len(sizes), max(sizes)
    forward, inverse = transform_matrices(rows)
    blocks = (groups, rows, LANES)
    spectra = (groups, 2 * rows, LANES)
    dma = pltpu.SemaphoreType.DMA
    anywhere = pl.BlockSpec(memory_space=pl.ANY)
    in_vmem = pl.BlockSpec(memory_space=pltpu.VMEM)
    return pl.pallas_call(
        functools.partial(layer_kernel, sizes),
        out_shape=pltpu.VMEM((rows, columns), bf16),
        in_specs=[anywhere] * 4 + [in_vmem] + [anywhere] * 3,
        out_specs=in_vmem,
        scratch_shapes=[
            pltpu.VMEM((rows, channels), bf16),
            pltpu.VMEM((rows, channels), bf16),
            pltpu.VMEM((rows, channels), bf16),
            pltpu.VMEM((4, channels, columns), bf16),
            pltpu.VMEM((2 * rows, rows), bf16),
            pltpu.VMEM((rows, 2 * rows), bf16),
            pltpu.VMEM(blocks, bf16),
            pltpu.VMEM(blocks, bf16),
            pltpu.VMEM(blocks, bf16),
            pltpu.VMEM(spectra, f32),
            pltpu.VMEM(spectra, f32),
            pltpu.VMEM((2 * rows, groups * LANES), bf16),
            pltpu.VMEM(blocks, bf16),
            pltpu.VMEM(blocks, bf16),
            pltpu.VMEM((chunk, channels), bf16),
            pltpu.VMEM((2, rows, columns), f32),
            pltpu.VMEM((2, rows, columns), bf16),
            pltpu.VMEM((2, rows, columns), bf16),
            pltpu.VMEM((rows, columns), bf16),
            pltpu.VMEM((rows, columns), bf16),
            dma((10,)),
            dma((groups,)),
            dma((groups,)),
            dma((groups,)),
            dma((groups,)),
            dma((chunks, groups)),
            dma((chunks, groups)),
            dma((2 * chunks,)),
            dma((2 * chunks,)),
            dma((chunks,)),
            dma((chunks,)),
        ],
        compiler_params=pltpu.CompilerParams(
            collective_id=0, has_side_effects=True, vmem_limit_bytes=56 * 1024 * 1024
        ),
        name="layer",
    )(
        gate_query, key_input, value_input, long_filter, skip_gain[None, :], out_weight,
        jnp.asarray(forward), jnp.asarray(inverse),
    )


def chunk_sizes(rows):
    return tuple(rows * part // sum(PARTS) for part in PARTS)


def groups_fit(block, weight, chans):
    rows, channels = block
    return (
        lax.axis_size("seq") == 8
        and chans == 4
        and channels == 8 * LANES
        and rows % 256 == 0
        and rows <= 512
        and weight[1] % (4 * LANES) == 0
        and weight[1] <= 4096
    )


def shards(gate_query, key_input, value_input, long_filter, skip_gain, out_weight):
    chans = lax.axis_size("chan")
    if groups_fit(gate_query.shape, out_weight.shape, chans):
        return fused(
            gate_query, key_input, value_input, long_filter, skip_gain, out_weight, chunk_sizes(gate_query.shape[0])
        )
    signal = (key_input.astype(f32) * value_input.astype(f32)).astype(bf16)
    conv = convolve(signal, long_filter)
    gated = (
        gate_query.astype(f32) * (conv + skip_gain[None, :] * signal.astype(f32))
    ).astype(bf16)
    summed = lax.psum_scatter(
        lax.dot_general(
            out_weight, gated, (((0,), (1,)), ((), ())), preferred_element_type=f32
        ).astype(bf16),
        "chan",
        scatter_dimension=0,
        tiled=True,
    )
    return summed.T.astype(bf16)


def solution(mesh):
    placed = (
        P("seq", "chan"),
        P("seq", "chan"),
        P("seq", "chan"),
        P("seq", "chan"),
        P("chan"),
        P("chan", None),
    )
    return jax.shard_map(
        shards, mesh=mesh, in_specs=placed, out_specs=P("seq", "chan"), check_vma=False
    )
```
